32 devices in a mesh: grp: 2 (over y), wide: 4 (over z), patch: 2 (over x), sub: 2 (over core).
Axes of the slice: x: 2, y: 2, z: 4, core: 2. Of those that a mesh axis runs over, the one named last changes fastest.
Arguments:
- survey: bfloat16 [512, 20, 729], P('wide', ('grp', 'patch')), parts along dimension 1, may hold values from -34 to 34
- test_matrix: bfloat16 [625, 48], replicated, may hold values from -6 to 6
Outputs:
- restored: float32 [512, 20, 729], P('wide', ('grp', 'patch')), parts along dimension 1
The draws below stay inside these ranges and needn't reach their ends.
There are 2 independent parts, one for each index of `grp`. The reference program is written for one: setup_inputs(seed, part) draws one part's arguments, and reference() takes and returns one part's arrays. A program takes and returns all parts, laid end to end along the dimension named above; an argument that names none is the same for every part. Nothing has to cross between parts.
All inputs are finite; a program needn't handle non-finite values.
Results may differ from the reference program's by a relative error of at most 0.0014.
Values may be sent and summed in bfloat16 or wider, within the bound.
No kernel may reach another device: no remote copies, remote signals or barrier semaphores. Data moves between devices by JAX's collectives and lax.ppermute only.
A program may use at most 64 MiB of HBM per device.

```python
import math
import jax
import jax.numpy as jnp
from jax import lax

LH = 5
RANK = 48
NT = 512
PS = 9
ORDER = 625
TR3 = 729
NF = 4
NXS = 10
N_PATCH = 2


def draw_survey(key, part):
    streams = jax.random.split(key, 6)
    moments = jnp.arange(NT, dtype=jnp.float32)[:, None, None]
    planes = jnp.arange(NXS, dtype=jnp.float32)[None, :, None]
    traces = jnp.arange(TR3, dtype=jnp.int32)
    middle = (PS - 1) / 2.0
    across_one = (traces // (PS * PS)).astype(jnp.float32)[None, None, :] - middle
    across_two = (traces // PS % PS).astype(jnp.float32)[None, None, :] - middle
    across_three = (traces % PS).astype(jnp.float32)[None, None, :] - middle
    polarity = jnp.where(jax.random.bernoulli(streams[0], 0.5, (16,)), 1.0, -1.0)
    amplitude = polarity * jax.random.uniform(streams[1], (16,), minval=0.5, maxval=1.5)
    noise_part = jnp.clip(0.7 * jax.random.normal(streams[5], (NT, NXS, TR3)), -2.8, 2.8)
    slopes = jax.random.uniform(streams[2], (16, 4), minval=-1.0, maxval=1.0)
    onsets = jax.random.uniform(streams[3], (16,), minval=0.0, maxval=float(NT))
    centres = jax.random.uniform(streams[4], (16,), minval=0.3, maxval=0.7) * (NF / NT)
    signal = noise_part
    for event_index in range(16):
        delays = moments - onsets[event_index] - slopes[event_index, 0] * planes
        delays = delays - slopes[event_index, 1] * across_one - slopes[event_index, 2] * across_two - slopes[event_index, 3] * across_three
        wrapped = jnp.mod(delays + NT / 2.0, float(NT)) - NT / 2.0
        spread = (math.pi * centres[event_index] * wrapped) ** 2
        signal = signal + amplitude[event_index] * (1.0 - 2.0 * spread) * jnp.exp(-spread)
    return signal.astype(jnp.bfloat16)


def noise(rng, dims, width, reach, kind=jnp.bfloat16):
    result = width * jax.random.normal(rng, dims, jnp.float32)
    return jnp.clip(result, min=-reach, max=reach).astype(kind)


def setup_inputs(seed: int = 0, part: int = 0) -> dict:
    key_of = jax.random.split(jax.random.key(seed), 3)
    own_keys = jax.random.split(jax.random.fold_in(key_of[2], part), 3)
    return {
        "survey": draw_survey(jax.random.fold_in(jax.random.fold_in(key_of[2], part), 71), part),
        "test_matrix": noise(key_of[1], (ORDER, RANK), 1.0, 6.0),
    }


DAMP = 0.5
HIGHEST = lax.Precision.HIGHEST

def level_weight():
    planes = jnp.arange(PS, dtype=jnp.int32)
    return jnp.minimum(jnp.minimum(planes + 1, PS - planes), LH).astype(jnp.float32)

def average_counts():
    weight = level_weight()
    return weight[:, None, None, None] * weight[None, :, None, None] * weight[None, None, :, None] * weight[None, None, None, :]

def phases(time_total, freq_total):
    frequency = jnp.arange(freq_total, dtype=jnp.int32) + 1
    moments = jnp.arange(time_total, dtype=jnp.int32)
    turned = frequency[:, None] * moments[None, :] % time_total
    return turned.astype(jnp.float32) * (2.0 * math.pi / time_total)

def forward_table(time_total, freq_total):
    angles = phases(time_total, freq_total)
    factor = 1.0 / math.sqrt(time_total)
    matrix = jnp.stack([jnp.cos(angles) * factor, -jnp.sin(angles) * factor], 1)
    return matrix.reshape(2 * freq_total, time_total).astype(jnp.bfloat16)

def inverse_table(time_total, freq_total):
    angles = phases(time_total, freq_total)
    factor = 2.0 / math.sqrt(time_total)
    matrix = jnp.stack([jnp.cos(angles) * factor, -jnp.sin(angles) * factor], 1)
    return matrix.reshape(2 * freq_total, time_total)

def spatial_fft(values):
    return jnp.fft.fftn(values, axes=(-4, -3, -2, -1))

def spatial_ifft(values):
    return jnp.fft.ifftn(values, axes=(-4, -3, -2, -1))

def padded(values):
    shaped = values.reshape(values.shape[:-1] + (LH, LH, LH, LH))
    return jnp.pad(shaped, [(0, 0)] * (shaped.ndim - 4) + [(0, LH - 1)] * 4)

def leading(values):
    corner = values[..., :LH, :LH, :LH, :LH]
    return corner.reshape(corner.shape[:-4] + (ORDER,))

def gram_of(matrix):
    return jnp.dot(matrix.astype(jnp.float32), matrix.T.astype(jnp.float32), precision=HIGHEST, preferred_element_type=jnp.float32)

def reduce_frequency(spectrum, test_hat):
    data_hat = spatial_fft(spectrum[0] + 1j * spectrum[1])
    sketch = leading(spatial_ifft(data_hat[None] * jnp.conj(test_hat)))
    real_part = jnp.real(sketch)
    imag_part = jnp.imag(sketch)
    basis_rows = jnp.concatenate([jnp.concatenate([real_part, imag_part], 1), jnp.concatenate([-imag_part, real_part], 1)], 0)
    gram_matrix = gram_of(basis_rows)
    factor = jnp.linalg.cholesky(gram_matrix)
    orthonormal = jax.scipy.linalg.solve_triangular(factor, basis_rows, lower=True).astype(jnp.bfloat16)
    orthonormal = lax.optimization_barrier(orthonormal).astype(jnp.float32)
    joined = orthonormal[:, :ORDER] + 1j * orthonormal[:, ORDER:]
    joined_hat = spatial_fft(padded(joined))
    coupled = leading(spatial_ifft(data_hat[None] * jnp.conj(joined_hat)))
    direct = jnp.real(coupled)
    twisted = -jnp.imag(coupled)
    damping = gram_of(direct) + gram_of(twisted)
    damp_level = DAMP * jnp.trace(damping) / (2 * RANK)
    shifted = damping + damp_level * jnp.eye(2 * RANK, dtype=jnp.float32)
    kernel = jax.scipy.linalg.cho_solve((jnp.linalg.cholesky(shifted), True), damping)
    coeffs = jnp.dot(kernel.astype(jnp.float32), direct.astype(jnp.float32), precision=HIGHEST, preferred_element_type=jnp.float32).astype(jnp.bfloat16)
    coeffs = lax.optimization_barrier(coeffs).astype(jnp.float32)
    summed = spatial_ifft(lax.optimization_barrier(jnp.sum(joined_hat * spatial_fft(padded(coeffs)), 0)))
    return jnp.stack([jnp.real(summed), jnp.imag(summed)], 0) / average_counts()

def reference(survey, test_matrix):
    forward = forward_table(NT, NF)
    inverse = inverse_table(NT, NF)
    test_grid = test_matrix.astype(jnp.float32).T
    test_hat = spatial_fft(padded(test_grid))
    extended = jnp.concatenate([survey, survey[:, :LH - 1, :]], 1)
    taper_weights = level_weight() / LH

    def one_patch(patch_index):
        window = lax.dynamic_slice_in_dim(extended, patch_index * LH, PS, 1)
        spectra = jnp.dot(forward.astype(jnp.float32), window.reshape(NT, PS * TR3).astype(jnp.float32), preferred_element_type=jnp.float32).astype(jnp.bfloat16)
        spectra = lax.optimization_barrier(spectra).astype(jnp.float32).reshape(NF, 2, PS, PS, PS, PS)
        averaged = lax.map(lambda spectrum: reduce_frequency(spectrum, test_hat), spectra)
        smooth = averaged.reshape(NF, 2, PS, TR3) * taper_weights[None, None, :, None]
        series = lax.dot_general(inverse.astype(jnp.float32), smooth.reshape(2 * NF, PS * TR3).astype(jnp.float32), (((0,), (0,)), ((), ())), precision=HIGHEST, preferred_element_type=jnp.float32)
        return series.reshape(NT, PS, TR3)
    patches = lax.map(one_patch, jnp.arange(N_PATCH, dtype=jnp.int32))
    carried = jnp.roll(patches[:, :, LH:, :], 1, axis=0)
    owned_planes = patches[:, :, :LH, :]
    merged = jnp.concatenate([owned_planes[:, :, :LH - 1, :] + carried, owned_planes[:, :, LH - 1:, :]], 2)
    return jnp.transpose(merged, (1, 0, 2, 3)).reshape(NT, NXS, TR3)
```

```python
import math

import jax
import jax.numpy as jnp
import numpy as np
from jax import lax
from jax.experimental import pallas as pl
from jax.experimental.pallas import tpu as pltpu
from jax.sharding import PartitionSpec as P

LH = 5
RANK = 48
PS = 9
TR3 = 729
DAMP = 0.5
HIGHEST = lax.Precision.HIGHEST

L2 = LH * LH
L3 = LH * L2
PS2 = PS * PS
BLK = 128
LANES = 768
SLAB = 8
PAIRS = (L2 + 1) // 2
KW = 512
F32 = jnp.float32
BF16 = jnp.bfloat16


def off2(i):
    return (i // LH) * PS + i % LH


def tables(wide, time_local):
    total = wide * time_local
    freq = np.arange(wide)[:, None] + 1
    turned = freq * np.arange(total)[None, :] % total
    angles = turned.astype(np.float64) * (2.0 * math.pi / total)
    waves = np.stack([np.cos(angles), -np.sin(angles)], 1) / math.sqrt(total)
    waves = waves.reshape(wide, 2, wide, time_local)
    owner = np.arange(wide)[:, None]
    turn = np.arange(wide)[None, :]
    ahead = (owner + turn) % wide
    behind = (owner - turn) % wide
    forward = waves[ahead, :, owner].reshape(wide, 2 * wide, time_local)
    back = 2.0 * waves[behind, :, owner]
    spread = np.zeros((wide, wide, 2, SLAB, LH, time_local))
    for plane in range(LH):
        spread[:, :, :, plane, plane, :] = back
    spread = spread.reshape(wide, wide * 2 * SLAB, LH * time_local)
    return forward.astype(jnp.bfloat16), spread.astype(np.float32)


def final_scale():
    planes = np.arange(PS)
    count = np.minimum(np.minimum(planes + 1, PS - planes), LH).astype(np.float64)
    cube = count[:, None, None] * count[None, :, None] * count[None, None, :]
    scale = np.zeros((1, LANES), np.float32)
    scale[0, :TR3] = 1.0 / (LH * cube.reshape(-1))
    return scale


def lane_targets():
    target = np.full((1, BLK), -1, np.int32)
    for jy in range(LH):
        for j2 in range(L2):
            target[0, jy * L2 + j2] = jy * PS2 + off2(j2)
    return target


def prepare_kernel(target_ref, test_ref, select_ref, rows_ref):
    row = lax.broadcasted_iota(jnp.int32, (KW, BLK), 0)
    place = row - target_ref[...]
    valid = jnp.broadcast_to(target_ref[...], (KW, BLK)) >= 0
    place = jnp.where(valid, place, -1)
    for i2 in range(2 * PAIRS):
        if i2 < L2:
            hot = jnp.where(place == off2(i2), 1.0, 0.0).astype(BF16)
        else:
            hot = jnp.zeros((KW, BLK), BF16)
        select_ref[:, i2 * BLK : (i2 + 1) * BLK] = hot
    test = test_ref[...].astype(F32)
    lane = lax.broadcasted_iota(jnp.int32, (RANK, BLK), 1)
    for ja in range(LH):
        if ja < LH - 1:
            piece = test[:, ja * L3 : ja * L3 + BLK]
        else:
            piece = jnp.concatenate([test[:, ja * L3 :], jnp.zeros((RANK, BLK - L3), F32)], 1)
        rows_ref[:, ja * BLK : (ja + 1) * BLK] = jnp.where(lane < L3, piece, 0.0).astype(BF16)


def dot_nn(a, b, precision=None):
    return lax.dot_general(
        a, b, (((1,), (0,)), ((), ())), precision=precision, preferred_element_type=F32
    )


def dot_nt(a, b, precision=None):
    return lax.dot_general(
        a, b, (((1,), (1,)), ((), ())), precision=precision, preferred_element_type=F32
    )


def dot_tn(a, b, precision=None):
    return lax.dot_general(
        a, b, (((0,), (0,)), ((), ())), precision=precision, preferred_element_type=F32
    )


def hermitian_gram(re, im):
    right = jnp.concatenate([re, im], 1)
    left = jnp.concatenate([right, jnp.concatenate([im, -re], 1)], 0)
    right = jnp.concatenate([right, jnp.zeros((BLK - RANK, right.shape[1]), F32)], 0)
    both = dot_nt(left, right, HIGHEST)
    return both[:RANK], both[RANK:]


def eliminate(are, aim, full):
    half = BLK // 2
    row = lax.broadcasted_iota(jnp.int32, (RANK, BLK), 0)
    lane = lax.broadcasted_iota(jnp.int32, (RANK, BLK), 1)
    are = are + jnp.where(lane == row + half, 1.0, 0.0)
    scales = []
    for p in range(RANK):
        rre = are[p : p + 1]
        rim = aim[p : p + 1]
        pivot = jnp.broadcast_to(are[p : p + 1, p : p + 1], (1, BLK))
        inverse = 1.0 / pivot
        rre = rre * inverse
        rim = rim * inverse
        cre = jnp.broadcast_to(are[:, p : p + 1], (RANK, BLK))
        cim = jnp.broadcast_to(aim[:, p : p + 1], (RANK, BLK))
        if full:
            nre = are - (cre * rre - cim * rim)
            nim = aim - (cre * rim + cim * rre)
            are = jnp.where(row == p, rre, nre)
            aim = jnp.where(row == p, rim, nim)
        else:
            cre = jnp.where(row > p, cre, 0.0)
            cim = jnp.where(row > p, cim, 0.0)
            scales.append(pivot)
            are, aim = are - (cre * rre - cim * rim), aim - (cre * rim + cim * rre)
    ore = are[:, half : half + RANK]
    oim = aim[:, half : half + RANK]
    if full:
        return ore, oim
    scale = lax.rsqrt(jnp.concatenate(scales, 0))[:, :RANK]
    return ore * scale, oim * scale


def real_form(re, im):
    return jnp.concatenate([jnp.concatenate([re, -im], 1), jnp.concatenate([im, re], 1)], 0)


def reduce_kernel(own_ref, next_ref, rows_ref, select_ref, scale_ref, stay_ref, move_ref, wide_ref, half_ref, hot_ref):
    own = own_ref[...].astype(F32)
    after = next_ref[...].astype(F32)
    pad = jnp.zeros((2 * SLAB - PS, LANES), F32)
    grid = []
    for e in range(2):
        grid += [own[e * SLAB : e * SLAB + LH], after[e * SLAB : e * SLAB + PS - LH], pad]
    grid = jnp.concatenate(grid, 0)
    shifted = []
    for iy in range(LH):
        turned = grid if iy == 0 else pltpu.roll(grid, LANES - iy * PS2, 1)
        shifted.append(turned[:, :KW].astype(BF16))
    shifted = jnp.concatenate(shifted, 0)
    blank = jnp.zeros((SLAB, BLK), F32)
    for a in range(2 * PS):
        wide_ref[a * BLK + BLK - SLAB : (a + 1) * BLK, :] = blank
    step = 2 * SLAB
    for pair in range(PAIRS):
        made = dot_nn(shifted, select_ref[:, pair * 2 * BLK : (pair + 1) * 2 * BLK])
        for within in range(2):
            i2 = 2 * pair + within
            if i2 < L2:
                for iy in range(LH):
                    for e in range(2):
                        top = (iy * 2 + e) * step
                        wide_ref[pl.ds(e * PS * BLK + iy * L2 + i2, PS, stride=BLK), :] = made[
                            top : top + PS, within * BLK : (within + 1) * BLK
                        ]
    for e in range(2):
        half_ref[:, e * BLK : (e + 1) * BLK] = wide_ref[e * PS * BLK : (e + 1) * PS * BLK, :].astype(BF16)

    def hankel(rows):
        out = []
        for ia in range(LH):
            out.append(dot_nn(rows, half_ref[ia * BLK : (ia + LH) * BLK, :]))
        return out

    parts = hankel(rows_ref[...])
    sre = jnp.concatenate([part[:, :BLK] for part in parts], 1)
    sim = jnp.concatenate([part[:, BLK:] for part in parts], 1)
    gre, gim = hermitian_gram(sre, sim)
    lre, lim = eliminate(gre, gim, False)
    basis = dot_nn(real_form(lre, lim), jnp.concatenate([sre, sim], 0), HIGHEST).astype(BF16)
    parts = hankel(basis)
    cre = jnp.concatenate([part[:RANK, :BLK] + part[RANK:, BLK:] for part in parts], 1)
    cim = jnp.concatenate([part[:RANK, BLK:] - part[RANK:, :BLK] for part in parts], 1)
    mre, mim = hermitian_gram(cre, cim)
    row = lax.broadcasted_iota(jnp.int32, (RANK, BLK), 0)
    lane = lax.broadcasted_iota(jnp.int32, (RANK, BLK), 1)
    diagonal = jnp.where(row == lane, mre, 0.0)
    level = jnp.sum(jnp.sum(diagonal, 1, keepdims=True), 0, keepdims=True) * (DAMP / RANK)
    ire, iim = eliminate(mre + jnp.where(row == lane, level, 0.0), mim, True)
    eye = jnp.where(row == lane, 1.0, 0.0)[:, :RANK]
    small = level[:, :1]
    kernel = real_form(eye - small * ire, -small * iim)
    coeffs = dot_nn(kernel, jnp.concatenate([cre, cim], 0), HIGHEST)
    fre = coeffs[:RANK].astype(BF16)
    fim = coeffs[RANK:].astype(BF16)
    wide_ref[...] = jnp.zeros((2 * PS * BLK, BLK), F32)
    for ja in range(LH):
        here = slice(ja * BLK, (ja + 1) * BLK)
        right = jnp.concatenate(
            [
                jnp.concatenate([fre[:, here], fim[:, here]], 1),
                jnp.concatenate([-fim[:, here], fre[:, here]], 1),
            ],
            0,
        )
        rebuilt = dot_tn(basis, right)
        for e in range(2):
            there = slice((e * PS + ja) * BLK, (e * PS + ja + LH) * BLK)
            wide_ref[there, :] = wide_ref[there, :] + rebuilt[:, e * BLK : (e + 1) * BLK]
    rest = jnp.zeros((step - PS, BLK), F32)
    for i2 in range(L2):
        cols = slice(i2 * BLK, (i2 + 1) * BLK)
        for iy in range(LH):
            for e in range(2):
                top = (iy * 2 + e) * step
                taken = wide_ref[pl.ds(e * PS * BLK + iy * L2 + i2, PS, stride=BLK), :]
                taken = jnp.concatenate([taken, rest], 0)
                high = taken.astype(BF16)
                hot_ref[top : top + step, cols] = high
                low = (taken - high.astype(F32)).astype(BF16)
                hot_ref[2 * LH * step + top : 2 * LH * step + top + step, cols] = low
    spans = dot_nt(hot_ref[...], select_ref[:, : L2 * BLK])
    spans = spans[: 2 * LH * step] + spans[2 * LH * step :]
    spans = jnp.concatenate([spans, jnp.zeros((2 * LH * step, LANES - KW), F32)], 1)
    total = spans[: 2 * step]
    for iy in range(1, LH):
        total = total + pltpu.roll(spans[iy * 2 * step : (iy + 1) * 2 * step], iy * PS2, 1)
    total = total * scale_ref[...]
    fill = jnp.zeros((SLAB - LH, LANES), F32)
    for e in range(2):
        top = e * step
        stay_ref[e * SLAB : (e + 1) * SLAB, :] = jnp.concatenate([total[top : top + LH], fill], 0)
        move_ref[e * SLAB : (e + 1) * SLAB, :] = jnp.concatenate(
            [total[top + LH : top + PS], jnp.zeros((2 * SLAB - PS - (SLAB - LH), LANES), F32)], 0
        )


def forward_kernel(owner_ref, survey_ref, table_ref, *out_refs):
    table = table_ref[owner_ref[0]]
    fill = jnp.zeros((1, LANES - TR3), F32)
    for plane in range(LH):
        waves = dot_nt(table, survey_ref[plane])
        for turn, out_ref in enumerate(out_refs):
            for e in range(2):
                at = 2 * turn + e
                line = jnp.concatenate([waves[at : at + 1], fill], 1)
                out_ref[e * SLAB + plane : e * SLAB + plane + 1, :] = line
    for out_ref in out_refs:
        for e in range(2):
            out_ref[e * SLAB + LH : (e + 1) * SLAB, :] = jnp.zeros((SLAB - LH, LANES), F32)


def inverse_kernel(owner_ref, table_ref, *refs):
    out_ref = refs[-1]
    time_local = out_ref.shape[2]
    waves = jnp.concatenate([ref[...] for ref in refs[:-1]], 0)
    table = table_ref[owner_ref[0]]
    series = dot_tn(waves, table, HIGHEST)
    for plane in range(LH):
        out_ref[plane] = series[:TR3, plane * time_local : (plane + 1) * time_local]


def vmem():
    return pl.BlockSpec(memory_space=pltpu.MemorySpace.VMEM)


def smem():
    return pl.BlockSpec(memory_space=pltpu.MemorySpace.SMEM)


def shifted(x, axis, by):
    devices = lax.axis_size(axis)
    return lax.ppermute(x, axis, [(i, (i + by) % devices) for i in range(devices)])


def shards(survey, test_matrix):
    wide = lax.axis_size("wide")
    time_local = survey.shape[0]
    forward, spread = tables(wide, time_local)
    owner = lax.axis_index("wide").astype(jnp.int32).reshape(1)
    slab = jax.ShapeDtypeStruct((2 * SLAB, LANES), F32)
    select, rows = pl.pallas_call(
        prepare_kernel,
        out_shape=(
            jax.ShapeDtypeStruct((KW, 2 * PAIRS * BLK), BF16),
            jax.ShapeDtypeStruct((RANK, LH * BLK), BF16),
        ),
        in_specs=[vmem(), vmem()],
        out_specs=(vmem(), vmem()),
        name="prepare",
    )(jnp.asarray(lane_targets()), test_matrix.T)
    partial = pl.pallas_call(
        forward_kernel,
        out_shape=[slab] * wide,
        in_specs=[smem(), vmem(), vmem()],
        out_specs=[vmem()] * wide,
        name="forward",
    )(owner, jnp.transpose(survey, (1, 2, 0)), jnp.asarray(forward))
    total = partial[0]
    for turn in range(1, wide):
        total = total + shifted(partial[turn], "wide", turn)
    own = total.astype(BF16)
    after = shifted(own, "patch", -1)
    stay, move = pl.pallas_call(
        reduce_kernel,
        out_shape=[slab, slab],
        in_specs=[vmem()] * 5,
        out_specs=[vmem(), vmem()],
        scratch_shapes=[
            pltpu.VMEM((2 * PS * BLK, BLK), F32),
            pltpu.VMEM((PS * BLK, 2 * BLK), BF16),
            pltpu.VMEM((4 * LH * 2 * SLAB, L2 * BLK), BF16),
        ],
        name="reduce",
    )(own, after, rows, select, jnp.asarray(final_scale()))
    smooth = stay + shifted(move, "patch", 1)
    gathered = [smooth] + [shifted(smooth, "wide", turn) for turn in range(1, wide)]
    series = pl.pallas_call(
        inverse_kernel,
        out_shape=jax.ShapeDtypeStruct((LH, TR3, time_local), F32),
        in_specs=[smem()] + [vmem()] * (1 + wide),
        out_specs=vmem(),
        name="inverse",
    )(owner, jnp.asarray(spread), *gathered)
    return jnp.transpose(series, (2, 0, 1))


def solution(mesh):
    return jax.shard_map(
        shards,
        mesh=mesh,
        in_specs=(P("wide", ("grp", "patch"), None), P()),
        out_specs=P("wide", ("grp", "patch"), None),
        check_vma=False,
    )
```

```python
import math

import jax
import jax.numpy as jnp
import numpy as np
from jax import lax
from jax.experimental import pallas as pl
from jax.experimental.pallas import tpu as pltpu
from jax.sharding import PartitionSpec as P

LH = 5
RANK = 48
PS = 9
TR3 = 729
DAMP = 0.5
HIGHEST = lax.Precision.HIGHEST

L2 = LH * LH
L3 = LH * L2
PS2 = PS * PS
BLK = 128
LANES = 768
SLAB = 8
GROUPS = L2 // SLAB
KW = 416
F32 = jnp.float32
BF16 = jnp.bfloat16


def off2(i):
    return (i // LH) * PS + i % LH


def slots():
    order = np.full((BLK, 2), -1, np.int32)
    for inner in range(L2):
        for iy in range(LH):
            if inner < GROUPS * SLAB:
                at = (inner // SLAB * LH + iy) * SLAB + inner % SLAB
            else:
                at = GROUPS * LH * SLAB + iy
            order[at] = iy, inner
    return order


def tables(wide, time_local):
    total = wide * time_local
    freq = np.arange(wide)[:, None] + 1
    turned = freq * np.arange(total)[None, :] % total
    angles = turned.astype(np.float64) * (2.0 * math.pi / total)
    waves = np.stack([np.cos(angles), -np.sin(angles)], 1) / math.sqrt(total)
    waves = waves.reshape(wide, 2, wide, time_local)
    owner = np.arange(wide)[:, None]
    turn = np.arange(wide)[None, :]
    forward = waves[(owner + turn) % wide, :, owner].reshape(wide, 2 * wide, time_local)
    inverse = waves[(owner - turn) % wide, :, owner].reshape(wide, 2 * wide, time_local)
    return forward.astype(jnp.bfloat16), (2.0 * inverse).astype(np.float32)


def final_scale():
    planes = np.arange(PS)
    count = np.minimum(np.minimum(planes + 1, PS - planes), LH).astype(np.float64)
    cube = count[:, None, None] * count[None, :, None] * count[None, None, :]
    scale = np.zeros((1, LANES), np.float32)
    scale[0, :TR3] = 1.0 / (LH * cube.reshape(-1))
    return scale


def lane_targets():
    order = slots()
    target = np.full((SLAB, BLK), -1, np.int32)
    used = order[:, 0] >= 0
    target[0, used] = order[used, 0] * PS2 + off2(order[used, 1])
    target[1, used] = order[used, 0] * L2 + order[used, 1]
    return target


def prepare_kernel(target_ref, test_ref, select_ref, rows_ref):
    target = target_ref[0:1, :]
    row = lax.broadcasted_iota(jnp.int32, (KW, BLK), 0)
    wanted = jnp.broadcast_to(target, (KW, BLK))
    place = jnp.where(wanted >= 0, row - wanted, -1)
    for i2 in range(L2):
        hot = jnp.where(place == off2(i2), 1.0, 0.0).astype(BF16)
        select_ref[:, i2 * BLK : (i2 + 1) * BLK] = hot
    test = test_ref[...].astype(F32)
    source = jnp.broadcast_to(target_ref[1:2, :], (BLK, BLK))
    spread = jnp.where(lax.broadcasted_iota(jnp.int32, (BLK, BLK), 0) == source, 1.0, 0.0).astype(BF16)
    for ja in range(LH):
        if ja < LH - 1:
            piece = test[:, ja * L3 : ja * L3 + BLK]
        else:
            piece = jnp.concatenate([test[:, ja * L3 :], jnp.zeros((RANK, BLK - L3), F32)], 1)
        rows_ref[:, ja * BLK : (ja + 1) * BLK] = dot_nn(piece.astype(BF16), spread).astype(BF16)


def dot_nn(a, b, precision=None):
    return lax.dot_general(
        a, b, (((1,), (0,)), ((), ())), precision=precision, preferred_element_type=F32
    )


def dot_nt(a, b, precision=None):
    return lax.dot_general(
        a, b, (((1,), (1,)), ((), ())), precision=precision, preferred_element_type=F32
    )


def dot_tn(a, b, precision=None):
    return lax.dot_general(
        a, b, (((0,), (0,)), ((), ())), precision=precision, preferred_element_type=F32
    )


def halves(x):
    high = x.astype(BF16)
    return high, (x - high.astype(F32)).astype(BF16)


def complex_gram(real):
    width = jnp.zeros((RANK, BLK - RANK), F32)
    re = real[:RANK, :RANK] + real[RANK:, RANK:]
    im = real[RANK:, :RANK] - real[:RANK, RANK:]
    return jnp.concatenate([re, width], 1), jnp.concatenate([im, width], 1)


def inverse_factor(are, aim):
    half = BLK // 2
    row = lax.broadcasted_iota(jnp.int32, (RANK, BLK), 0)
    lane = lax.broadcasted_iota(jnp.int32, (RANK, BLK), 1)
    are = are + jnp.where(lane == row + half, 1.0, 0.0)
    tiles = RANK // SLAB
    are = [are[t * SLAB : (t + 1) * SLAB] for t in range(tiles)]
    aim = [aim[t * SLAB : (t + 1) * SLAB] for t in range(tiles)]
    sub = lax.broadcasted_iota(jnp.int32, (SLAB, BLK), 0)
    scales = []
    for p in range(RANK):
        own, at = p // SLAB, p % SLAB
        cre = [jnp.broadcast_to(are[t][:, p : p + 1], (SLAB, BLK)) for t in range(own, tiles)]
        cim = [jnp.broadcast_to(aim[t][:, p : p + 1], (SLAB, BLK)) for t in range(own, tiles)]
        pivot = cre[0][at : at + 1]
        scales.append(pivot)
        inverse = 1.0 / pivot
        rre = jnp.broadcast_to(are[own][at : at + 1] * inverse, (SLAB, BLK))
        rim = jnp.broadcast_to(aim[own][at : at + 1] * inverse, (SLAB, BLK))
        below = sub > at
        cre[0] = jnp.where(below, cre[0], 0.0)
        cim[0] = jnp.where(below, cim[0], 0.0)
        for t in range(own, tiles):
            if t == own and at == SLAB - 1:
                continue
            fre, fim = cre[t - own], cim[t - own]
            are[t], aim[t] = are[t] - (fre * rre - fim * rim), aim[t] - (fre * rim + fim * rre)
    scale = lax.rsqrt(jnp.concatenate(scales, 0))[:, :RANK]
    ore = jnp.concatenate(are, 0)[:, half : half + RANK]
    oim = jnp.concatenate(aim, 0)[:, half : half + RANK]
    return ore * scale, oim * scale


def real_form(re, im):
    return jnp.concatenate([jnp.concatenate([re, -im], 1), jnp.concatenate([im, re], 1)], 0)


def swap_tiles(tiles):
    turned = jnp.transpose(jnp.stack(tiles, 0), (1, 0, 2))
    return [turned[k] for k in range(SLAB)]


def reduce_kernel(own_ref, next_ref, rows_ref, select_ref, scale_ref, stay_ref, move_ref, half_ref, full_ref, hot_ref):
    own = own_ref[...].astype(F32)
    after = next_ref[...].astype(F32)
    tile = jnp.zeros((SLAB, BLK), F32)
    first, last = [], []
    for e in range(2):
        top = e * SLAB
        grid = jnp.concatenate([own[top : top + LH], after[top : top + SLAB - LH]], 0)
        final = after[top + SLAB - LH : top + PS - LH]
        first.append([grid if iy == 0 else pltpu.roll(grid, LANES - iy * PS2, 1) for iy in range(LH)])
        shifts = [final] + [pltpu.roll(final, LANES - iy * PS2, 1) for iy in range(1, LH)]
        last.append(jnp.concatenate(shifts + [jnp.zeros((SLAB - LH, LANES), F32)], 0))
    lines = [first[e][iy] for iy in range(LH) for e in range(2)] + last
    lines = jnp.concatenate(lines, 0)[:, :KW].astype(BF16)
    waiting = {}

    def place(a, e, t, value):
        if t % 2 == 0:
            waiting[a, e] = value
        else:
            both = jnp.concatenate([waiting.pop((a, e)), value], 0).astype(BF16)
            top = a * BLK + (t - 1) * SLAB
            half_ref[top : top + 2 * SLAB, e * BLK : (e + 1) * BLK] = both

    for group in range(GROUPS):
        made = dot_nn(lines, select_ref[:, group * SLAB * BLK : (group + 1) * SLAB * BLK])
        for e in range(2):
            for iy in range(LH):
                top = (iy * 2 + e) * SLAB
                taken = [made[top : top + SLAB, k * BLK : (k + 1) * BLK] for k in range(SLAB)]
                for a, value in enumerate(swap_tiles(taken)):
                    place(a, e, group * LH + iy, value)
            top = (2 * LH + e) * SLAB
            taken = [made[top : top + SLAB, k * BLK : (k + 1) * BLK] for k in range(SLAB)]
            for iy, value in enumerate(swap_tiles(taken)[:LH]):
                place(PS - 1, e, group * LH + iy, value)
    made = dot_nn(lines, select_ref[:, GROUPS * SLAB * BLK :])
    for e in range(2):
        taken = [made[(iy * 2 + e) * SLAB : (iy * 2 + e + 1) * SLAB] for iy in range(LH)]
        for a, value in enumerate(swap_tiles(taken + [tile] * (SLAB - LH))):
            place(a, e, GROUPS * LH, value)
        place(PS - 1, e, GROUPS * LH, made[(2 * LH + e) * SLAB : (2 * LH + e + 1) * SLAB])

    def hankel(rows):
        return [dot_nn(rows, half_ref[ia * BLK : (ia + LH) * BLK, :]) for ia in range(LH)]

    parts = hankel(rows_ref[...])
    sketch = jnp.concatenate(
        [
            jnp.concatenate([part[:, :BLK] for part in parts], 1),
            jnp.concatenate([part[:, BLK:] for part in parts], 1),
        ],
        0,
    )
    lre, lim = inverse_factor(*complex_gram(dot_nt(sketch, sketch, HIGHEST)))
    basis = dot_nn(real_form(lre, lim), sketch, HIGHEST).astype(BF16)
    parts = hankel(basis)
    coupled = jnp.concatenate(
        [
            jnp.concatenate([part[:RANK, :BLK] + part[RANK:, BLK:] for part in parts], 1),
            jnp.concatenate([part[:RANK, BLK:] - part[RANK:, :BLK] for part in parts], 1),
        ],
        0,
    )
    high, low = halves(coupled)
    mre, mim = complex_gram(dot_nt(high, high) + dot_nt(high, low) + dot_nt(low, high))
    row = lax.broadcasted_iota(jnp.int32, (RANK, BLK), 0)
    lane = lax.broadcasted_iota(jnp.int32, (RANK, BLK), 1)
    diagonal = jnp.where(row == lane, mre, 0.0)
    level = jnp.sum(jnp.sum(diagonal, 1, keepdims=True), 0, keepdims=True) * (DAMP / RANK)
    lre, lim = inverse_factor(mre + jnp.where(row == lane, level, 0.0), mim)
    left = jnp.concatenate([lre, lim], 0)
    right = jnp.concatenate([jnp.concatenate([lre, lim], 1), jnp.concatenate([lim, -lre], 1)], 0)
    inverse = dot_tn(left, right, HIGHEST) * level[:, :1]
    eye = jnp.where(row == lane, 1.0, 0.0)[:, :RANK]
    khigh, klow = halves(real_form(eye - inverse[:, :RANK], -inverse[:, RANK:]))
    coeffs = dot_nn(khigh, high) + dot_nn(khigh, low) + dot_nn(klow, high)
    fre = coeffs[:RANK].astype(BF16)
    fim = coeffs[RANK:].astype(BF16)
    gap = jnp.zeros((BLK - 2 * RANK, BLK), BF16)
    columns = [
        jnp.transpose(jnp.concatenate([basis[:, ia * BLK : (ia + 1) * BLK], gap], 0))
        for ia in reversed(range(LH))
    ]
    columns = jnp.concatenate(columns, 1)
    gap = jnp.zeros((BLK - 2 * RANK, 2 * BLK), BF16)
    weights = []
    for ja in range(LH):
        here = slice(ja * BLK, (ja + 1) * BLK)
        weights.append(jnp.concatenate([fre[:, here], fim[:, here]], 1))
        weights.append(jnp.concatenate([-fim[:, here], fre[:, here]], 1))
        weights.append(gap)
    weights = jnp.concatenate(weights, 0)
    for a in range(PS):
        most, least = min(a, LH - 1), max(0, a - LH + 1)
        left = columns[:, (LH - 1 - most) * BLK : (LH - least) * BLK]
        right = weights[(a - most) * BLK : (a - least + 1) * BLK]
        full_ref[a * BLK : (a + 1) * BLK, :] = dot_nn(left, right)

    def tile_of(a, e, t):
        top = a * BLK + t * SLAB
        return full_ref[top : top + SLAB, e * BLK : (e + 1) * BLK]

    def put(line, inner, pair):
        cols = slice(inner * BLK, (inner + 1) * BLK)
        hot_ref[line * 2 * SLAB : (line + 1) * 2 * SLAB, cols] = jnp.concatenate(pair, 0).astype(BF16)

    for group in range(GROUPS):
        for iy in range(LH):
            t = group * LH + iy
            swapped = [swap_tiles([tile_of(a, e, t) for a in range(SLAB)]) for e in range(2)]
            for k in range(SLAB):
                put(iy, group * SLAB + k, [swapped[0][k], swapped[1][k]])
        swapped = []
        for e in range(2):
            taken = [tile_of(PS - 1, e, group * LH + iy) for iy in range(LH)]
            swapped.append(swap_tiles(taken + [tile] * (SLAB - LH)))
        for k in range(SLAB):
            put(LH, group * SLAB + k, [swapped[0][k], swapped[1][k]])
    t = GROUPS * LH
    swapped = [swap_tiles([tile_of(a, e, t) for a in range(SLAB)]) for e in range(2)]
    for iy in range(LH):
        put(iy, L2 - 1, [swapped[0][iy], swapped[1][iy]])
    put(LH, L2 - 1, [tile_of(PS - 1, e, t) for e in range(2)])
    spans = dot_nt(hot_ref[...], select_ref[...])
    spans = jnp.concatenate([spans, jnp.zeros((2 * (LH + 1) * SLAB, LANES - KW), F32)], 1)
    sub = lax.broadcasted_iota(jnp.int32, (SLAB, LANES), 0)
    for e in range(2):
        total = spans[e * SLAB : (e + 1) * SLAB]
        for iy in range(1, LH):
            top = (2 * iy + e) * SLAB
            total = total + pltpu.roll(spans[top : top + SLAB], iy * PS2, 1)
        top = (2 * LH + e) * SLAB
        final = spans[top : top + 1]
        for iy in range(1, LH):
            final = final + pltpu.roll(spans[top + iy : top + iy + 1], iy * PS2, 1)
        total = total * scale_ref[...]
        final = jnp.broadcast_to(final * scale_ref[...], (SLAB, LANES))
        stay_ref[e * SLAB : (e + 1) * SLAB, :] = jnp.where(sub < LH, total, 0.0)
        moved = pltpu.roll(total, SLAB - LH, 0)
        moved = jnp.where(sub < SLAB - LH, moved, jnp.where(sub == SLAB - LH, final, 0.0))
        move_ref[e * SLAB : (e + 1) * SLAB, :] = moved


def scratches():
    return [
        pltpu.VMEM((PS * BLK, 2 * BLK), BF16),
        pltpu.VMEM((PS * BLK, 2 * BLK), F32),
        pltpu.VMEM((2 * (LH + 1) * SLAB, L2 * BLK), BF16),
    ]


def forward_kernel(owner_ref, survey_ref, table_ref, *out_refs):
    table = table_ref[owner_ref[0]]
    fill = jnp.zeros((1, LANES - TR3), F32)
    for plane in range(LH):
        waves = dot_nt(table, survey_ref[plane])
        for turn, out_ref in enumerate(out_refs):
            for e in range(2):
                at = 2 * turn + e
                line = jnp.concatenate([waves[at : at + 1], fill], 1)
                out_ref[e * SLAB + plane : e * SLAB + plane + 1, :] = line
    for out_ref in out_refs:
        for e in range(2):
            out_ref[e * SLAB + LH : (e + 1) * SLAB, :] = jnp.zeros((SLAB - LH, LANES), F32)


def inverse_kernel(owner_ref, table_ref, *refs):
    out_ref, lines_ref, sems = refs[-3:]
    planes, traces, time_local = out_ref.shape
    waves = jnp.concatenate([ref[...] for ref in refs[:-3]], 0)
    count = waves.shape[0]
    high = waves.astype(BF16).astype(F32)
    lines = jnp.transpose(jnp.concatenate([high, waves - high], 0)).astype(BF16)[:traces]
    lines = jnp.concatenate([lines, lines], 1)
    table = table_ref[owner_ref[0]]
    sub = lax.broadcasted_iota(jnp.int32, (SLAB, time_local), 0)
    copies = []
    for plane in range(planes):
        spread = []
        for line in range(count // SLAB):
            values = jnp.broadcast_to(table[line : line + 1], (SLAB, time_local))
            spread.append(jnp.where(sub == plane, values, 0.0))
        thigh, tlow = halves(jnp.concatenate(spread, 0))
        weights = jnp.concatenate([thigh, thigh, tlow, jnp.zeros_like(tlow)], 0)
        lines_ref[plane] = dot_nn(lines, weights)
        copy = pltpu.make_async_copy(lines_ref.at[plane], out_ref.at[plane], sems.at[plane])
        copy.start()
        copies.append(copy)
    for copy in copies:
        copy.wait()


def vmem():
    return pl.BlockSpec(memory_space=pltpu.MemorySpace.VMEM)


def smem():
    return pl.BlockSpec(memory_space=pltpu.MemorySpace.SMEM)


def shifted(x, axis, by):
    devices = lax.axis_size(axis)
    return lax.ppermute(x, axis, [(i, (i + by) % devices) for i in range(devices)])


def shards(survey, test_matrix):
    wide = lax.axis_size("wide")
    time_local = survey.shape[0]
    forward, inverse = tables(wide, time_local)
    owner = lax.axis_index("wide").astype(jnp.int32).reshape(1)
    slab = jax.ShapeDtypeStruct((2 * SLAB, LANES), F32)
    select, rows = pl.pallas_call(
        prepare_kernel,
        out_shape=(
            jax.ShapeDtypeStruct((KW, L2 * BLK), BF16),
            jax.ShapeDtypeStruct((RANK, LH * BLK), BF16),
        ),
        in_specs=[vmem(), vmem()],
        out_specs=(vmem(), vmem()),
        name="prepare",
    )(jnp.asarray(lane_targets()), test_matrix.T)
    partial = pl.pallas_call(
        forward_kernel,
        out_shape=[slab] * wide,
        in_specs=[smem(), vmem(), vmem()],
        out_specs=[vmem()] * wide,
        name="forward",
    )(owner, jnp.transpose(survey, (1, 2, 0)), jnp.asarray(forward))
    total = partial[0]
    for turn in range(1, wide):
        total = total + shifted(partial[turn], "wide", turn)
    own = total.astype(BF16)
    after = shifted(own, "patch", -1)
    stay, move = pl.pallas_call(
        reduce_kernel,
        out_shape=[slab, slab],
        in_specs=[vmem()] * 5,
        out_specs=[vmem(), vmem()],
        scratch_shapes=scratches(),
        name="reduce",
    )(own, after, rows, select, jnp.asarray(final_scale()))
    smooth = stay + shifted(move, "patch", 1)
    gathered = [smooth] + [shifted(smooth, "wide", turn) for turn in range(1, wide)]
    series = pl.pallas_call(
        inverse_kernel,
        out_shape=jax.ShapeDtypeStruct((LH, TR3, time_local), F32),
        in_specs=[smem()] + [vmem()] * (1 + wide),
        out_specs=pl.BlockSpec(memory_space=pl.ANY),
        scratch_shapes=[pltpu.VMEM((LH, TR3, time_local), F32), pltpu.SemaphoreType.DMA((LH,))],
        name="inverse",
    )(owner, jnp.asarray(inverse), *gathered)
    return jnp.transpose(series, (2, 0, 1))


def solution(mesh):
    return jax.shard_map(
        shards,
        mesh=mesh,
        in_specs=(P("wide", ("grp", "patch"), None), P()),
        out_specs=P("wide", ("grp", "patch"), None),
        check_vma=False,
    )
```

```python
import math

import jax
import jax.numpy as jnp
import numpy as np
from jax import lax
from jax.experimental import pallas as pl
from jax.experimental.pallas import tpu as pltpu
from jax.sharding import PartitionSpec as P

LH = 5
RANK = 48
PS = 9
TR3 = 729
DAMP = 0.5
HIGHEST = lax.Precision.HIGHEST

L2 = LH * LH
L3 = LH * L2
PS2 = PS * PS
BLK = 128
LANES = 768
SLAB = 8
GROUPS = L2 // SLAB
PANEL = 8
TRAIL = 8
KW = 416
F32 = jnp.float32
BF16 = jnp.bfloat16


def off2(i):
    return (i // LH) * PS + i % LH


def partner(place, turn, wide):
    if wide & (wide - 1) == 0:
        return place ^ turn
    return (place + turn) % wide


def sending_turns(wide):
    turns = list(range(wide - 1, -1, -1))
    return [turns, turns[:2][::-1] + turns[2:]]


def returning_turns(wide):
    turns = list(range(wide))
    return [turns, turns[:-2] + turns[-2:][::-1]]


def tables(wide, time_local):
    total = wide * time_local
    freq = np.arange(wide)[:, None] + 1
    turned = freq * np.arange(total)[None, :] % total
    angles = turned.astype(np.float64) * (2.0 * math.pi / total)
    waves = np.stack([np.cos(angles), -np.sin(angles)], 1) / math.sqrt(total)
    waves = waves.reshape(wide, 2, wide, time_local)
    owner = np.arange(wide)[:, None]
    ahead = np.array([[partner(w, turn, wide) for turn in range(wide)] for w in range(wide)])
    behind = np.argsort(ahead, 0)
    forward = [waves[ahead[:, turns], :, owner] for turns in sending_turns(wide)]
    forward = np.stack(forward, 0).reshape(2 * wide, 2 * wide, time_local)
    inverse = waves[behind, :, owner].reshape(wide, 2 * wide, time_local)
    return forward.astype(jnp.bfloat16), (2.0 * inverse).astype(np.float32)


def final_scale():
    planes = np.arange(PS)
    count = np.minimum(np.minimum(planes + 1, PS - planes), LH).astype(np.float64)
    cube = count[:, None, None] * count[None, :, None] * count[None, None, :]
    scale = np.zeros((1, LANES), np.float32)
    scale[0, :TR3] = 1.0 / (LH * cube.reshape(-1))
    return scale


def count_from(x, step, most):
    total = jnp.zeros_like(x)
    for k in range(1, most + 1):
        total = total + jnp.where(x >= k * step, 1, 0)
    return total


def lane_slots(shape):
    lane = lax.broadcasted_iota(jnp.int32, shape, 1)
    group = count_from(lane, LH * SLAB, GROUPS - 1)
    inside = lane - group * (LH * SLAB)
    iy = count_from(inside, SLAB, LH - 1)
    inner = group * SLAB + inside - iy * SLAB
    rest = lane >= GROUPS * LH * SLAB
    iy = jnp.where(rest, lane - GROUPS * LH * SLAB, iy)
    inner = jnp.where(rest, L2 - 1, inner)
    return iy, inner, iy < LH


def fill_select(select_ref):
    iy, inner, valid = lane_slots((KW, BLK))
    row = lax.broadcasted_iota(jnp.int32, (KW, BLK), 0)
    high = count_from(inner, LH, LH - 1)
    place = row - iy * PS2 - high * PS - (inner - high * LH)
    place = jnp.where(valid, place, -1)
    for i2 in range(L2):
        hot = jnp.where(place == off2(i2), 1.0, 0.0).astype(BF16)
        select_ref[:, i2 * BLK : (i2 + 1) * BLK] = hot


def fill_rows(test, rows_ref):
    iy, inner, valid = lane_slots((BLK, BLK))
    source = jnp.where(valid, iy * L2 + inner, -1)
    spread = jnp.where(lax.broadcasted_iota(jnp.int32, (BLK, BLK), 0) == source, 1.0, 0.0).astype(BF16)
    for ja in range(LH):
        if ja < LH - 1:
            piece = test[:, ja * L3 : ja * L3 + BLK]
        else:
            piece = jnp.concatenate([test[:, ja * L3 :], jnp.zeros((RANK, BLK - L3), F32)], 1)
        rows_ref[:, ja * BLK : (ja + 1) * BLK] = dot_nn(piece.astype(BF16), spread).astype(BF16)


def dot_nn(a, b, precision=None):
    return lax.dot_general(
        a, b, (((1,), (0,)), ((), ())), precision=precision, preferred_element_type=F32
    )


def dot_nt(a, b, precision=None):
    return lax.dot_general(
        a, b, (((1,), (1,)), ((), ())), precision=precision, preferred_element_type=F32
    )


def dot_tn(a, b, precision=None):
    return lax.dot_general(
        a, b, (((0,), (0,)), ((), ())), precision=precision, preferred_element_type=F32
    )


def halves(x):
    high = x.astype(BF16)
    return high, (x - high.astype(F32)).astype(BF16)


def thirds(x):
    first = x.astype(BF16)
    rest = x - first.astype(F32)
    second = rest.astype(BF16)
    return first, second, (rest - second.astype(F32)).astype(BF16)


def precise(dot, left, right):
    rows = left[0].shape[0]
    one = dot(jnp.concatenate(left, 0), right[0])
    two = dot(jnp.concatenate(left[:2], 0), right[1])
    low = one[2 * rows :] + two[rows:] + dot(left[0], right[2])
    return one[:rows] + (one[rows : 2 * rows] + two[:rows] + low)


def complex_gram(real):
    width = jnp.zeros((RANK, BLK - RANK), F32)
    re = real[:RANK, :RANK] + real[RANK:, RANK:]
    im = real[RANK:, :RANK] - real[:RANK, RANK:]
    return jnp.concatenate([re, width], 1), jnp.concatenate([im, width], 1)


def inverse_factor(are, aim):
    half = BLK // 2
    row = lax.broadcasted_iota(jnp.int32, (RANK, BLK), 0)
    lane = lax.broadcasted_iota(jnp.int32, (RANK, BLK), 1)
    are = are + jnp.where(lane == row + half, 1.0, 0.0)
    tiles = RANK // SLAB
    are = [are[t * SLAB : (t + 1) * SLAB] for t in range(tiles)]
    aim = [aim[t * SLAB : (t + 1) * SLAB] for t in range(tiles)]
    sub = lax.broadcasted_iota(jnp.int32, (SLAB, BLK), 0)

    def columns_of(t, first, count):
        found = []
        for p in range(first, first + count):
            found.append(
                (
                    jnp.broadcast_to(are[t][:, p : p + 1], (SLAB, BLK)),
                    jnp.broadcast_to(aim[t][:, p : p + 1], (SLAB, BLK)),
                )
            )
        return found

    def row_of(x, k):
        return jnp.broadcast_to(x[k : k + 1], (SLAB, BLK))

    def less(x, column, line):
        xre, xim = x
        cre, cim = column
        rre, rim = line
        return xre - (cre * rre - cim * rim), xim - (cre * rim + cim * rre)

    pivots = [jnp.ones((SLAB, BLK), F32)] * tiles
    for first in range(0, RANK, PANEL):
        own = first // SLAB
        columns = {own: columns_of(own, first, PANEL)}
        for k in range(PANEL):
            if k % TRAIL == 0:
                for t in range(own + 1, tiles):
                    columns[t] = [None] * k + columns_of(t, first + k, TRAIL)
            at = (first + k) % SLAB
            pivot = row_of(columns[own][k][0], at)
            inverse = 1.0 / pivot
            pivots[own] = jnp.where(sub == at, pivot, pivots[own])
            lead = {t: columns[t][k] for t in range(own, tiles)}
            lead[own] = tuple(jnp.where(sub > at, x, 0.0) for x in lead[own])
            for j in range(k + 1, PANEL):
                line = [row_of(x, at) * inverse for x in columns[own][j]]
                for t in range(own, tiles):
                    if j < len(columns[t]):
                        columns[t][j] = less(columns[t][j], lead[t], line)
            line = [row_of(x, at) * inverse for x in (are[own], aim[own])]
            for t in range(own, tiles):
                if t > own or at < SLAB - 1:
                    are[t], aim[t] = less((are[t], aim[t]), lead[t], line)
    scales = [lax.rsqrt(pivot) for pivot in pivots]
    scale = jnp.concatenate(scales, 0)[:, :RANK]
    ore = jnp.concatenate(are, 0)[:, half : half + RANK]
    oim = jnp.concatenate(aim, 0)[:, half : half + RANK]
    return ore * scale, oim * scale


def real_form(re, im):
    return jnp.concatenate([jnp.concatenate([re, -im], 1), jnp.concatenate([im, re], 1)], 0)


def swap_tiles(tiles):
    turned = jnp.transpose(jnp.stack(tiles, 0), (1, 0, 2))
    return [turned[k] for k in range(SLAB)]


def reduce_kernel(mine_ref, other_ref, rows_ref, select_ref, scale_ref, out_ref, half_ref, full_ref, hot_ref):
    first_role = lax.axis_index("sub") == 0
    mine = mine_ref[...].astype(F32)
    other = other_ref[...].astype(F32)
    own = jnp.where(first_role, mine, other)
    after = jnp.where(first_role, other, mine)
    tile = jnp.zeros((SLAB, BLK), F32)
    first, last = [], []
    for e in range(2):
        top = e * SLAB
        grid = jnp.concatenate([own[top : top + LH], after[top : top + SLAB - LH]], 0)
        final = after[top + SLAB - LH : top + PS - LH]
        first.append([grid if iy == 0 else pltpu.roll(grid, LANES - iy * PS2, 1) for iy in range(LH)])
        shifts = [final] + [pltpu.roll(final, LANES - iy * PS2, 1) for iy in range(1, LH)]
        last.append(jnp.concatenate(shifts + [jnp.zeros((SLAB - LH, LANES), F32)], 0))
    lines = [first[e][iy] for iy in range(LH) for e in range(2)] + last
    lines = jnp.concatenate(lines, 0)[:, :KW].astype(BF16)
    waiting = {}

    def place(a, e, t, value):
        if t % 2 == 0:
            waiting[a, e] = value
        else:
            both = jnp.concatenate([waiting.pop((a, e)), value], 0).astype(BF16)
            top = a * BLK + (t - 1) * SLAB
            half_ref[top : top + 2 * SLAB, e * BLK : (e + 1) * BLK] = both

    for group in range(GROUPS):
        made = dot_nn(lines, select_ref[:, group * SLAB * BLK : (group + 1) * SLAB * BLK])
        for e in range(2):
            for iy in range(LH):
                top = (iy * 2 + e) * SLAB
                taken = [made[top : top + SLAB, k * BLK : (k + 1) * BLK] for k in range(SLAB)]
                for a, value in enumerate(swap_tiles(taken)):
                    place(a, e, group * LH + iy, value)
            top = (2 * LH + e) * SLAB
            taken = [made[top : top + SLAB, k * BLK : (k + 1) * BLK] for k in range(SLAB)]
            for iy, value in enumerate(swap_tiles(taken)[:LH]):
                place(PS - 1, e, group * LH + iy, value)
    made = dot_nn(lines, select_ref[:, GROUPS * SLAB * BLK :])
    for e in range(2):
        taken = [made[(iy * 2 + e) * SLAB : (iy * 2 + e + 1) * SLAB] for iy in range(LH)]
        for a, value in enumerate(swap_tiles(taken + [tile] * (SLAB - LH))):
            place(a, e, GROUPS * LH, value)
        place(PS - 1, e, GROUPS * LH, made[(2 * LH + e) * SLAB : (2 * LH + e + 1) * SLAB])

    def hankel(rows):
        return [dot_nn(rows, half_ref[ia * BLK : (ia + LH) * BLK, :]) for ia in range(LH)]

    parts = hankel(rows_ref[...])
    sketch = jnp.concatenate(
        [
            jnp.concatenate([part[:, :BLK] for part in parts], 1),
            jnp.concatenate([part[:, BLK:] for part in parts], 1),
        ],
        0,
    )
    split = thirds(sketch)
    lre, lim = inverse_factor(*complex_gram(precise(dot_nt, split, split)))
    basis = precise(dot_nn, thirds(real_form(lre, lim)), split).astype(BF16)
    parts = hankel(basis)
    coupled = jnp.concatenate(
        [
            jnp.concatenate([part[:RANK, :BLK] + part[RANK:, BLK:] for part in parts], 1),
            jnp.concatenate([part[:RANK, BLK:] - part[RANK:, :BLK] for part in parts], 1),
        ],
        0,
    )
    high, low = halves(coupled)
    both = dot_nt(jnp.concatenate([high, low], 0), high)
    mre, mim = complex_gram(both[: 2 * RANK] + (both[2 * RANK :] + dot_nt(high, low)))
    row = lax.broadcasted_iota(jnp.int32, (RANK, BLK), 0)
    lane = lax.broadcasted_iota(jnp.int32, (RANK, BLK), 1)
    diagonal = jnp.where(row == lane, mre, 0.0)
    level = jnp.sum(jnp.sum(diagonal, 1, keepdims=True), 0, keepdims=True) * (DAMP / RANK)
    lre, lim = inverse_factor(mre + jnp.where(row == lane, level, 0.0), mim)
    left = jnp.concatenate([lre, lim], 0)
    right = jnp.concatenate([jnp.concatenate([lre, lim], 1), jnp.concatenate([lim, -lre], 1)], 0)
    (lhigh, llow), (rhigh, rlow) = halves(left), halves(right)
    inverse = dot_tn(lhigh, rhigh) + (dot_tn(lhigh, rlow) + dot_tn(llow, rhigh))
    inverse = inverse * level[:, :1]
    eye = jnp.where(row == lane, 1.0, 0.0)[:, :RANK]
    khigh, klow = halves(real_form(eye - inverse[:, :RANK], -inverse[:, RANK:]))
    both = dot_nn(jnp.concatenate([khigh, klow], 0), high)
    coeffs = both[: 2 * RANK] + (both[2 * RANK :] + dot_nn(khigh, low))
    fre = coeffs[:RANK].astype(BF16)
    fim = coeffs[RANK:].astype(BF16)
    gap = jnp.zeros((BLK - 2 * RANK, BLK), BF16)
    columns = [
        jnp.transpose(jnp.concatenate([basis[:, ia * BLK : (ia + 1) * BLK], gap], 0))
        for ia in reversed(range(LH))
    ]
    columns = jnp.concatenate(columns, 1)
    gap = jnp.zeros((BLK - 2 * RANK, 2 * BLK), BF16)
    weights = []
    for ja in range(LH):
        here = slice(ja * BLK, (ja + 1) * BLK)
        weights.append(jnp.concatenate([fre[:, here], fim[:, here]], 1))
        weights.append(jnp.concatenate([-fim[:, here], fre[:, here]], 1))
        weights.append(gap)
    weights = jnp.concatenate(weights, 0)
    for a in range(PS):
        most, least = min(a, LH - 1), max(0, a - LH + 1)
        left = columns[:, (LH - 1 - most) * BLK : (LH - least) * BLK]
        right = weights[(a - most) * BLK : (a - least + 1) * BLK]
        full_ref[a * BLK : (a + 1) * BLK, :] = dot_nn(left, right)

    def tile_of(a, e, t):
        top = a * BLK + t * SLAB
        return full_ref[top : top + SLAB, e * BLK : (e + 1) * BLK]

    def put(line, inner, pair):
        cols = slice(inner * BLK, (inner + 1) * BLK)
        hot_ref[line * 2 * SLAB : (line + 1) * 2 * SLAB, cols] = jnp.concatenate(pair, 0).astype(BF16)

    for group in range(GROUPS):
        for iy in range(LH):
            t = group * LH + iy
            swapped = [swap_tiles([tile_of(a, e, t) for a in range(SLAB)]) for e in range(2)]
            for k in range(SLAB):
                put(iy, group * SLAB + k, [swapped[0][k], swapped[1][k]])
        swapped = []
        for e in range(2):
            taken = [tile_of(PS - 1, e, group * LH + iy) for iy in range(LH)]
            swapped.append(swap_tiles(taken + [tile] * (SLAB - LH)))
        for k in range(SLAB):
            put(LH, group * SLAB + k, [swapped[0][k], swapped[1][k]])
    t = GROUPS * LH
    swapped = [swap_tiles([tile_of(a, e, t) for a in range(SLAB)]) for e in range(2)]
    for iy in range(LH):
        put(iy, L2 - 1, [swapped[0][iy], swapped[1][iy]])
    put(LH, L2 - 1, [tile_of(PS - 1, e, t) for e in range(2)])
    spans = dot_nt(hot_ref[...], select_ref[...])
    spans = jnp.concatenate([spans, jnp.zeros((2 * (LH + 1) * SLAB, LANES - KW), F32)], 1)
    sub = lax.broadcasted_iota(jnp.int32, (SLAB, LANES), 0)
    for e in range(2):
        total = spans[e * SLAB : (e + 1) * SLAB]
        for iy in range(1, LH):
            top = (2 * iy + e) * SLAB
            total = total + pltpu.roll(spans[top : top + SLAB], iy * PS2, 1)
        top = (2 * LH + e) * SLAB
        final = spans[top : top + 1]
        for iy in range(1, LH):
            final = final + pltpu.roll(spans[top + iy : top + iy + 1], iy * PS2, 1)
        total = total * scale_ref[...]
        final = jnp.broadcast_to(final * scale_ref[...], (SLAB, LANES))
        stay = jnp.where(sub < LH, total, 0.0)
        moved = pltpu.roll(total, SLAB - LH, 0)
        moved = jnp.where(sub < SLAB - LH, moved, jnp.where(sub == SLAB - LH, final, 0.0))
        out_ref[e * SLAB : (e + 1) * SLAB, :] = jnp.where(first_role, stay, moved)


def scratches():
    return [
        pltpu.VMEM((PS * BLK, 2 * BLK), BF16),
        pltpu.VMEM((PS * BLK, 2 * BLK), F32),
        pltpu.VMEM((2 * (LH + 1) * SLAB, L2 * BLK), BF16),
    ]


def forward_kernel(survey_ref, table_ref, far_test, far_scale, *refs):
    out_refs, (select_ref, rows_ref, scale_ref) = refs[:-7], refs[-7:-4]
    planes_ref, waves_ref, test_ref, sems = refs[-4:]
    line = lax.axis_index("sub") * lax.axis_size("wide") + lax.axis_index("wide")
    pairs = (
        (survey_ref, planes_ref),
        (table_ref.at[line], waves_ref),
        (far_test, test_ref),
        (far_scale, scale_ref),
    )
    copies = [pltpu.make_async_copy(a, b, sems.at[k]) for k, (a, b) in enumerate(pairs)]
    for copy in copies:
        copy.start()
    for out_ref in out_refs:
        out_ref[...] = jnp.zeros(out_ref.shape, F32)
    fill_select(select_ref)
    for copy in copies[1:]:
        copy.wait()
    fill_rows(test_ref[...].astype(F32), rows_ref)
    table = waves_ref[...]
    copies[0].wait()
    planes = [dot_nt(table, planes_ref[plane]) for plane in range(planes_ref.shape[0])]
    for plane, waves in enumerate(planes):
        for turn, out_ref in enumerate(out_refs):
            for e in range(2):
                at = 2 * turn + e
                out_ref[e * SLAB + plane : e * SLAB + plane + 1, :TR3] = waves[at : at + 1]


def join_kernel(*refs):
    size = refs[0].shape[0]
    slabs = [ref[...] for ref in refs[:-1]]
    first_role = lax.axis_index("sub") == 0
    turned = [slabs[turn] for turn in returning_turns(len(slabs))[1]]
    for turn, (slab, other) in enumerate(zip(slabs, turned)):
        slab = slab if slab is other else jnp.where(first_role, slab, other)
        refs[-1][turn * size : (turn + 1) * size, :] = slab


def sum_kernel(*refs):
    total = refs[0][...]
    for ref in refs[1:-1]:
        total = total + ref[...]
    refs[-1][...] = total.astype(refs[-1].dtype)


def inverse_kernel(table_ref, mine_ref, other_ref, out_ref, lines_ref, sems):
    planes, traces, time_local = out_ref.shape
    waves = mine_ref[...] + other_ref[...]
    count = waves.shape[0]
    high = waves.astype(BF16).astype(F32)
    lines = jnp.transpose(jnp.concatenate([high, waves - high], 0)).astype(BF16)[:traces]
    lines = jnp.concatenate([lines, lines], 1)
    table = table_ref[lax.axis_index("wide")]
    sub = lax.broadcasted_iota(jnp.int32, (SLAB, time_local), 0)
    weights = []
    for plane in range(planes):
        spread = []
        for line in range(count // SLAB):
            values = jnp.broadcast_to(table[line : line + 1], (SLAB, time_local))
            spread.append(jnp.where(sub == plane, values, 0.0))
        thigh, tlow = halves(jnp.concatenate(spread, 0))
        weights.append(jnp.concatenate([thigh, thigh, tlow, jnp.zeros_like(tlow)], 0))
    copies = []
    for first in range(0, planes, 2):
        group = range(first, min(first + 2, planes))
        series = dot_nn(lines, jnp.concatenate([weights[plane] for plane in group], 1))
        for plane in group:
            start = (plane - first) * time_local
            lines_ref[plane] = series[:, start : start + time_local]
            copy = pltpu.make_async_copy(lines_ref.at[plane], out_ref.at[plane], sems.at[plane])
            copy.start()
            copies.append(copy)
    for copy in copies:
        copy.wait()


def vmem():
    return pl.BlockSpec(memory_space=pltpu.MemorySpace.VMEM)


def far():
    return pl.BlockSpec(memory_space=pltpu.MemorySpace.HBM)


def by_role(x, turns, step):
    axes = ("wide", "patch", "sub")
    wide, patches, members = [lax.axis_size(axis) for axis in axes]
    pairs = []
    for w in range(wide):
        for p in range(patches):
            for member in range(members):
                there = partner(w, turns[member], wide)
                target = p if member == 0 else (p + step) % patches
                source = (w * patches + p) * members + member
                pairs.append((source, (there * patches + target) * members + member))
    return lax.ppermute(x, axes, pairs)


def swapped(x):
    members = lax.axis_size("sub")
    return lax.ppermute(x, "sub", [(i, (i + 1) % members) for i in range(members)])


def held(x):
    return pltpu.with_memory_space_constraint(x, pltpu.MemorySpace.VMEM)


def room(mebibytes):
    return pltpu.CompilerParams(vmem_limit_bytes=mebibytes * 2**20)


def fixed(x):
    return pltpu.with_memory_space_constraint(x, pltpu.MemorySpace.HBM)


def near(shape, dtype):
    return pltpu.MemorySpace.VMEM(shape, dtype)


def small(kernel, parts, shape, dtype, name):
    return pl.pallas_call(
        kernel,
        out_shape=near(shape, dtype),
        in_specs=[vmem()] * len(parts),
        out_specs=vmem(),
        name=name,
        compiler_params=room(2),
    )(*[held(part) for part in parts])


def shards(survey, test_matrix):
    wide = lax.axis_size("wide")
    time_local, planes, traces = survey.shape
    forward, inverse = tables(wide, time_local)
    slab = near((2 * SLAB, LANES), F32)
    *partial, select, rows, scale = pl.pallas_call(
        forward_kernel,
        out_shape=[slab] * wide
        + [near((KW, L2 * BLK), BF16), near((RANK, LH * BLK), BF16), near((1, LANES), F32)],
        in_specs=[far()] * 4,
        out_specs=[vmem()] * (wide + 3),
        scratch_shapes=[
            pltpu.VMEM((planes, traces, time_local), BF16),
            pltpu.VMEM((2 * wide, time_local), BF16),
            pltpu.VMEM(test_matrix.shape[::-1], BF16),
            pltpu.SemaphoreType.DMA((4,)),
        ],
        name="forward",
        compiler_params=room(8),
    )(
        fixed(jnp.transpose(survey, (1, 2, 0))),
        fixed(jnp.asarray(forward)),
        fixed(test_matrix.T),
        fixed(jnp.asarray(final_scale())),
    )
    parts = [by_role(part, turns, -1) for part, turns in zip(partial, zip(*sending_turns(wide)))]
    mine = small(sum_kernel, parts, (2 * SLAB, LANES), BF16, "sum")
    result = pl.pallas_call(
        reduce_kernel,
        out_shape=slab,
        in_specs=[vmem()] * 5,
        out_specs=vmem(),
        scratch_shapes=scratches(),
        name="reduce",
        compiler_params=room(24),
    )(held(mine), held(swapped(mine)), held(rows), held(select), held(scale))
    parts = [by_role(result, turns, 1) for turns in zip(*returning_turns(wide))]
    mine = small(join_kernel, parts, (wide * 2 * SLAB, LANES), F32, "join")
    series = pl.pallas_call(
        inverse_kernel,
        out_shape=jax.ShapeDtypeStruct((planes, traces, time_local), F32),
        in_specs=[vmem()] * 3,
        out_specs=far(),
        scratch_shapes=[
            pltpu.VMEM((planes, traces, time_local), F32),
            pltpu.SemaphoreType.DMA((planes,)),
        ],
        name="inverse",
        compiler_params=room(16),
    )(jnp.asarray(inverse), held(mine), held(swapped(mine)))
    return jnp.transpose(series, (2, 0, 1))


def solution(mesh):
    return jax.shard_map(
        shards,
        mesh=mesh,
        in_specs=(P("wide", ("grp", "patch"), None), P()),
        out_specs=P("wide", ("grp", "patch"), None),
        check_vma=False,
    )
```
